128 devices in a mesh: ctx: 8 (over x_lo, z), fsdp: 16 (over y, x_hi, core).
Axes of the slice: x: 4 (x_hi: 2, x_lo: 2; x = x_hi * 2 + x_lo), y: 4, z: 4, core: 2. Of those that a mesh axis runs over, the one named last changes fastest.
Arguments:
- queries: bfloat16 [16, 1536, 2048], P('fsdp', 'ctx'), may hold values from -5 to 5
- keys: bfloat16 [16, 1536, 2048], P('fsdp', 'ctx'), may hold values from -5 to 5
- values: bfloat16 [16, 1536, 2048], P('fsdp', 'ctx'), may hold values from -6 to 6
- resid: float32 [16, 1536, 4096], P('fsdp', 'ctx'), may hold values from -6 to 6
- gate: float32 [16, 4096], P('fsdp'), may hold values from 0.5 to 1.5
- out_weight: bfloat16 [2048, 4096], P(('ctx', 'fsdp')), may hold values from -2 to 2
- conv_weight: float32 [3, 4096], replicated, may hold values from -2.5 to 2.5
- cotangent: float32 [16, 1536, 4096], P('fsdp', 'ctx'), may hold values from -6 to 6
Outputs:
- encoded: float32 [16, 1536, 4096], P('fsdp', 'ctx')
- grad_queries: bfloat16 [16, 1536, 2048], P('fsdp', 'ctx')
- grad_keys: bfloat16 [16, 1536, 2048], P('fsdp', 'ctx')
- grad_values: bfloat16 [16, 1536, 2048], P('fsdp', 'ctx')
- grad_conv: float32 [3, 4096], replicated
The draws below stay inside these ranges and needn't reach their ends.
All inputs are finite; a program needn't handle non-finite values.
Results may differ from the reference program's by a relative error of at most 0.019.
Values may be sent and summed in bfloat16 or wider, within the bound.
No kernel may reach another device: no remote copies, remote signals or barrier semaphores. Data moves between devices by JAX's collectives and lax.ppermute only.
A program may use at most 192 MiB of HBM per device.

```python
import math
import jax
import jax.numpy as jnp
from jax import lax

D = 4096
HEADS = 16
HDIM = 128
KSIZE = 3
TOKF = 48
HW = 2048
ROWS = 192
FRAMES = 32
SEQ = 1536
CLIPS = 16


def draw_pair(key):
    shape = (CLIPS, SEQ, HW)
    parts = jax.random.split(jax.random.fold_in(key, 7), 2)
    query_vals = jnp.clip(jax.random.normal(parts[0], shape, jnp.float32), -4.0, 4.0)
    key_vals = jnp.clip(jax.random.normal(parts[1], shape, jnp.float32), -4.0, 4.0)
    return (query_vals, key_vals)


def draw_queries(key, part):
    return draw_pair(key)[0].astype(jnp.bfloat16)


def draw_keys(key, part):
    return draw_pair(key)[1].astype(jnp.bfloat16)


def with_spikes(entries, stream_key, source, target, blocks, factor):
    owner, partner = [(jnp.arange(entries.shape[position]) // (entries.shape[position] // blocks)).reshape([-1 if axis == position else 1 for axis in range(entries.ndim)]) for position in (source, target)]
    chosen = jax.random.permutation(stream_key, blocks)[partner]
    strong = (owner == chosen) | (owner == (partner + blocks // 2) % blocks)
    return jnp.where(strong, factor * entries, entries)


def levels(key, shape, cuts, least, high):
    level, own = 1.0, jax.random.fold_in(key, 6)
    for dim, blocks in cuts:
        draws = jnp.exp(jax.random.uniform(jax.random.fold_in(own, dim), (blocks,), jnp.float32, least / len(cuts), high / len(cuts)))
        level = level * jnp.repeat(draws, shape[dim] // blocks).reshape([-1 if axis == dim else 1 for axis in range(len(shape))])
    return level


def scatter_about(stream_key, dims, width, reach, shards=(), dtype=jnp.bfloat16):
    gain = levels(stream_key, dims, shards, -0.22, 0.18) if shards else 1.0
    drawn = jax.random.normal(stream_key, dims, jnp.float32) * width * gain
    return jnp.minimum(jnp.maximum(drawn, -reach), reach).astype(dtype)


def noise_with(key, dims, spread, reach, cuts, heavy, kind=jnp.bfloat16):
    drawn = spread * jax.random.normal(key, dims, jnp.float32)
    if cuts:
        drawn = drawn * levels(key, dims, cuts, -0.22, 0.18)
    return jnp.clip(with_spikes(drawn, jax.random.fold_in(key, 3), *heavy), -reach, reach).astype(kind)


def setup_inputs(seed: int = 0) -> dict:
    seeds = jax.random.split(jax.random.key(seed), 9)
    queries = draw_queries(jax.random.fold_in(seeds[8], 71), 0)
    keys = draw_keys(jax.random.fold_in(seeds[8], 71), 0)
    values = scatter_about(seeds[2], (CLIPS, SEQ, HW), 1.0, 6.0, ((0, 16), (1, 8)))
    resid = scatter_about(seeds[3], (CLIPS, SEQ, D), 1.0, 6.0, ((0, 16), (1, 8)), jnp.float32)
    gate = jnp.clip(0.5 + 1.0 * jax.random.uniform(seeds[4], (CLIPS, D), jnp.float32) ** levels(seeds[4], (CLIPS, D), ((0, 16),), -0.2, 0.2), 0.5, 1.5)
    out_weight = scatter_about(seeds[5], (HW, D), 8 ** -0.5, 2.0, ((0, 128),))
    conv_weight = scatter_about(seeds[6], (KSIZE, D), 0.5, 2.5, (), jnp.float32)
    cotangent = noise_with(seeds[7], (CLIPS, SEQ, D), 1.0, 6.0, ((0, 16), (1, 8)), (1, 2, 8, 2.0), jnp.float32)
    return dict(queries=queries, keys=keys, values=values, resid=resid, gate=gate, out_weight=out_weight, conv_weight=conv_weight, cotangent=cotangent)


def head_view(array):
    return array.reshape(array.shape[0], HEADS, HDIM).astype(jnp.float32)

def round_low(array):
    return lax.optimization_barrier(array.astype(jnp.bfloat16)).astype(jnp.float32)

def forward_clip(operands):
    queries, keys, values = operands
    factor = 1.0 / math.sqrt(HDIM)
    query_f = head_view(queries)
    key_f = head_view(keys)
    value_f = head_view(values)
    scores = jnp.einsum('ihe,jhe->hij', query_f, key_f) * factor
    peak = lax.optimization_barrier(jnp.max(scores, axis=2, keepdims=True))
    raised = jnp.exp(scores - peak)
    totals = lax.optimization_barrier(jnp.sum(raised, axis=2, keepdims=True))
    weights = round_low(raised)
    summed = jnp.einsum('hij,jhe->ihe', weights, value_f)
    attended = (summed / jnp.transpose(totals, (1, 0, 2))).astype(jnp.bfloat16)
    log_totals = (peak + jnp.log(totals))[:, :, 0]
    return (attended.reshape(SEQ, HW), log_totals)

def backward_clip(operands):
    queries, keys, values, attended, grad_att, log_totals = operands
    factor = 1.0 / math.sqrt(HDIM)
    runs = SEQ // ROWS
    query_f = head_view(queries)
    key_f = head_view(keys)
    value_f = head_view(values)
    grad_f = head_view(grad_att)
    attended_f = head_view(attended)
    scores = jnp.einsum('ihe,jhe->hij', query_f, key_f) * factor
    probs = jnp.exp(scores - log_totals[:, :, None])
    probs_low = round_low(probs)
    value_parts = jnp.einsum('hbij,bihe->bjhe', probs_low.reshape(HEADS, runs, ROWS, SEQ), grad_f.reshape(runs, ROWS, HEADS, HDIM))
    grad_values = lax.optimization_barrier(jnp.sum(round_low(value_parts), axis=0)).astype(jnp.bfloat16)
    dprob = jnp.einsum('ihe,jhe->hij', grad_f, value_f)
    deltas = jnp.transpose(lax.optimization_barrier(jnp.sum(grad_f * attended_f, axis=2)))
    dscore = round_low(probs * (dprob - deltas[:, :, None]))
    grad_queries = (jnp.einsum('hij,jhe->ihe', dscore, key_f) * factor).astype(jnp.bfloat16)
    key_parts = jnp.einsum('hbij,bihe->bjhe', dscore.reshape(HEADS, runs, ROWS, SEQ), query_f.reshape(runs, ROWS, HEADS, HDIM)) * factor
    grad_keys = lax.optimization_barrier(jnp.sum(round_low(key_parts), axis=0)).astype(jnp.bfloat16)
    return (grad_queries.reshape(SEQ, HW), grad_keys.reshape(SEQ, HW), grad_values.reshape(SEQ, HW))

def reference(queries, keys, values, resid, gate, out_weight, conv_weight, cotangent):
    attended, log_totals = lax.map(forward_clip, (queries, keys, values))
    projected = jnp.dot(attended.reshape(CLIPS * SEQ, HW), out_weight, preferred_element_type=jnp.float32)
    projected = projected.reshape(CLIPS, SEQ, D)
    mixed = (resid + gate[:, None, :] * projected).astype(jnp.bfloat16)
    mixed_f = mixed.astype(jnp.float32).reshape(CLIPS, FRAMES, TOKF, D)
    padded = jnp.pad(mixed_f, ((0, 0), (KSIZE - 1, 0), (0, 0), (0, 0)))
    encoded = mixed_f
    for offset in range(KSIZE):
        begin = KSIZE - 1 - offset
        encoded = encoded + conv_weight[offset] * padded[:, begin:begin + FRAMES]
    encoded = encoded.reshape(CLIPS, SEQ, D)
    cot_frames = cotangent.reshape(CLIPS, FRAMES, TOKF, D)
    cot_padded = jnp.pad(cot_frames, ((0, 0), (0, KSIZE - 1), (0, 0), (0, 0)))
    grad_mixed = cot_frames
    grad_list = []
    for offset in range(KSIZE):
        grad_mixed = grad_mixed + conv_weight[offset] * cot_padded[:, offset:offset + FRAMES]
        begin = KSIZE - 1 - offset
        grad_list.append(lax.optimization_barrier(jnp.sum(cot_frames * padded[:, begin:begin + FRAMES], axis=(0, 1, 2))))
    grad_conv = jnp.stack(grad_list)
    grad_proj = (gate[:, None, :] * grad_mixed.reshape(CLIPS, SEQ, D)).astype(jnp.bfloat16)
    grad_att = lax.dot_general(grad_proj.reshape(CLIPS * SEQ, D), out_weight, (((1,), (1,)), ((), ())), preferred_element_type=jnp.float32)
    grad_att = grad_att.astype(jnp.bfloat16).reshape(CLIPS, SEQ, HW)
    grad_queries, grad_keys, grad_values = lax.map(backward_clip, (queries, keys, values, attended, grad_att, log_totals))
    return (encoded, grad_queries, grad_keys, grad_values, grad_conv)
```

```python
import math

import jax
import jax.numpy as jnp
import numpy as np
from jax import lax
from jax.experimental import pallas as pl
from jax.experimental.pallas import tpu as pltpu
from jax.sharding import PartitionSpec as P

HDIM = 128
KSIZE = 3
TOKF = 48
CTX = 8
ROWS = 192
SEQ = CTX * ROWS
HW = 2048
D = 4096
HALF = D // 2
SPAN = (KSIZE - 1) * TOKF
PIECE = HW // CTX
BLOCK = 256
FACTOR = 1.0 / math.sqrt(HDIM)
LOG2E = math.log2(math.e)
AXES = ("ctx", "fsdp")
bf16 = jnp.bfloat16
f32 = jnp.float32


def coords(flat):
    ctx, fsdp = divmod(flat, 16)
    x_lo, z = divmod(ctx, 4)
    y, rest = divmod(fsdp, 4)
    x_hi, core = divmod(rest, 2)
    return dict(x=x_hi * 2 + x_lo, y=y, z=z, core=core)


def flat_of(place):
    x_hi, x_lo = divmod(place["x"], 2)
    return (x_lo * 4 + place["z"]) * 16 + place["y"] * 4 + x_hi * 2 + place["core"]


def shift(array, dim, by):
    size = 2 if dim == "core" else 4
    pairs = []
    for source in range(128):
        place = coords(source)
        place[dim] = (place[dim] + by) % size
        pairs.append((source, flat_of(place)))
    return lax.ppermute(array, AXES, pairs)


def swap(array, axis, key):
    count = lax.axis_size(axis)
    return lax.ppermute(array, axis, [(i, i ^ key) for i in range(count)])


def along(array, by):
    pairs = [(i, i + by) for i in range(CTX) if 0 <= i + by < CTX]
    return lax.ppermute(array, "ctx", pairs)


def moved(offsets, dim, by):
    return [dict(o, **{dim: o[dim] - by}) for o in offsets]


def gather_rows(rows):
    got = [(rows, [dict(x=0, y=0, z=0)])]
    for by in (1, -1, 2):
        got.append((shift(rows, "z", by), moved(got[0][1], "z", by)))
    plane = jnp.concatenate([g[0] for g in got], axis=0)
    offs = [o for g in got for o in g[1]]
    got = [(plane, offs)]
    for by in (1, -1, 2):
        got.append((shift(plane, "x", by), moved(offs, "x", by)))
    low = jnp.concatenate([got[0][0], got[1][0]], axis=0)
    low_offs = got[0][1] + got[1][1]
    high = jnp.concatenate([got[2][0], got[3][0]], axis=0)
    high_offs = got[2][1] + got[3][1]
    low_p = shift(low, "y", 1)
    high_m = shift(high, "y", -1)
    high_p = shift(high, "y", 1)
    low_m = shift(low, "y", -1)
    low_2 = shift(low_p, "y", 1)
    high_2 = shift(high_m, "y", -1)
    return [
        (low, low_offs),
        (high, high_offs),
        (low_p, moved(low_offs, "y", 1)),
        (high_m, moved(high_offs, "y", -1)),
        (high_p, moved(high_offs, "y", 1)),
        (low_m, moved(low_offs, "y", -1)),
        (low_2, moved(low_offs, "y", 2)),
        (high_2, moved(high_offs, "y", -2)),
    ]


def params(mib=56):
    return pltpu.CompilerParams(vmem_limit_bytes=mib * 2**20)


SMEM = pl.BlockSpec(memory_space=pltpu.SMEM)
VMEM = pl.BlockSpec(memory_space=pltpu.VMEM)
ANY = pl.BlockSpec(memory_space=pl.ANY)


def shape(dims, dtype):
    return jax.ShapeDtypeStruct(dims, dtype)


def pack_body(ids, q_ref, k_ref, v_ref, *outs):
    for key in range(CTX):
        start = pl.multiple_of((ids[0] ^ key) * PIECE, PIECE)
        for place, ref in enumerate((q_ref, k_ref, v_ref)):
            outs[key][:, place * PIECE : (place + 1) * PIECE] = ref[:, pl.ds(start, PIECE)]


def pack(ids, queries, keys, values):
    return pl.pallas_call(
        pack_body,
        in_specs=[SMEM, VMEM, VMEM, VMEM],
        out_specs=[VMEM] * CTX,
        out_shape=[shape((ROWS, 3 * PIECE), bf16)] * CTX,
        compiler_params=params(),
        name="pack",
    )(ids, queries, keys, values)


def forward_body(*refs):
    pieces, refs = refs[:CTX], refs[CTX:]
    outs, refs = refs[:CTX], refs[CTX:]
    log_ref, q_s, k_s, v_s, o_s = refs
    for head in range(2):
        for key in range(CTX):
            rows = slice(key * ROWS, (key + 1) * ROWS)
            for place, ref in enumerate((q_s, k_s, v_s)):
                start = place * PIECE + head * HDIM
                ref[head, rows, :] = pieces[key][:, start : start + HDIM]

    for head in range(2):

        def step(index, carry):
            start = pl.multiple_of(index * BLOCK, BLOCK)
            query = q_s[head, pl.ds(start, BLOCK), :]
            scores = lax.dot_general(
                query, k_s[head], (((1,), (1,)), ((), ())), preferred_element_type=f32
            )
            peak = jnp.max(scores, axis=1, keepdims=True)
            raised = jnp.exp2((scores - peak) * (FACTOR * LOG2E))
            totals = jnp.sum(raised, axis=1, keepdims=True)
            summed = jnp.dot(raised.astype(bf16), v_s[head], preferred_element_type=f32)
            o_s[pl.ds(start, BLOCK), head * HDIM : (head + 1) * HDIM] = (summed / totals).astype(
                bf16
            )
            logs = peak * (FACTOR * LOG2E) + jnp.log2(totals)
            log_ref[head, :, pl.ds(start, BLOCK)] = jnp.broadcast_to(logs, (BLOCK, HDIM)).T[:8]
            return carry

        lax.fori_loop(0, SEQ // BLOCK, step, 0)
    for key in range(CTX):
        outs[key][...] = o_s[key * ROWS : (key + 1) * ROWS, :]


def forward(pieces):
    return pl.pallas_call(
        forward_body,
        in_specs=[VMEM] * CTX,
        out_specs=[VMEM] * (CTX + 1),
        out_shape=[shape((ROWS, PIECE), bf16)] * CTX + [shape((2, 8, SEQ), f32)],
        scratch_shapes=[pltpu.VMEM((2, SEQ, HDIM), bf16)] * 3 + [pltpu.VMEM((SEQ, PIECE), bf16)],
        compiler_params=params(),
        name="attend",
    )(*pieces)


def backward_body(head, *refs):
    pieces, refs = refs[:CTX], refs[CTX:]
    att, refs = refs[:CTX], refs[CTX:]
    grads, refs = refs[:CTX], refs[CTX:]
    log_ref, refs = refs[0], refs[1:]
    outs, refs = refs[:CTX], refs[CTX:]
    q_s, k_s, v_s, g_s, d_s, kt_s, dq_s, dk_s, dv_s = refs
    cols = slice(head * HDIM, (head + 1) * HDIM)
    for key in range(CTX):
        rows = slice(key * ROWS, (key + 1) * ROWS)
        for place, ref in enumerate((q_s, k_s, v_s)):
            start = place * PIECE + head * HDIM
            ref[rows, :] = pieces[key][:, start : start + HDIM]
        grad = grads[key][:, cols]
        g_s[rows, :] = grad
        d_s[rows, :] = grad.astype(f32) * att[key][:, cols].astype(f32)
    kt_s[...] = k_s[...].astype(f32).T.astype(bf16)
    dk_s[...] = jnp.zeros_like(dk_s)
    dv_s[...] = jnp.zeros_like(dv_s)
    wide = 512

    def step(index, carry):
        start = pl.multiple_of(index * BLOCK, BLOCK)
        query = q_s[pl.ds(start, BLOCK), :]
        grad = g_s[pl.ds(start, BLOCK), :]
        delta = jnp.sum(d_s[pl.ds(start, BLOCK), :].T, axis=0, keepdims=True)
        logs = log_ref[head, 0:1, pl.ds(start, BLOCK)]
        dq = jnp.zeros((HDIM, BLOCK), f32)
        for chunk in range(SEQ // wide):
            part = slice(chunk * wide, (chunk + 1) * wide)
            scores = lax.dot_general(
                k_s[part, :], query, (((1,), (1,)), ((), ())), preferred_element_type=f32
            )
            dprob = lax.dot_general(
                v_s[part, :], grad, (((1,), (1,)), ((), ())), preferred_element_type=f32
            )
            probs = jnp.exp2(scores * (FACTOR * LOG2E) - logs)
            dscore = (probs * (dprob - delta)).astype(bf16)
            dv_s[part, :] += jnp.dot(probs.astype(bf16), grad, preferred_element_type=f32)
            dk_s[part, :] += jnp.dot(dscore, query, preferred_element_type=f32)
            dq = dq + jnp.dot(kt_s[:, part], dscore, preferred_element_type=f32)
        dq_s[pl.ds(start, BLOCK), :] = (dq.T * FACTOR).astype(bf16)
        return carry

    lax.fori_loop(0, SEQ // BLOCK, step, 0)
    for key in range(CTX):
        rows = slice(key * ROWS, (key + 1) * ROWS)
        outs[key][:, 0:HDIM] = dq_s[rows, :]
        outs[key][:, HDIM : 2 * HDIM] = (dk_s[rows, :] * FACTOR).astype(bf16)
        outs[key][:, 2 * HDIM :] = dv_s[rows, :].astype(bf16)


def backward(head, pieces, att, grads, logs):
    return pl.pallas_call(
        lambda *refs: backward_body(head, *refs),
        in_specs=[VMEM] * (3 * CTX + 1),
        out_specs=[VMEM] * CTX,
        out_shape=[shape((ROWS, 3 * HDIM), bf16)] * CTX,
        scratch_shapes=[pltpu.VMEM((SEQ, HDIM), bf16)] * 4
        + [
            pltpu.VMEM((SEQ, HDIM), f32),
            pltpu.VMEM((HDIM, SEQ), bf16),
            pltpu.VMEM((SEQ, HDIM), bf16),
            pltpu.VMEM((SEQ, HDIM), f32),
            pltpu.VMEM((SEQ, HDIM), f32),
        ],
        compiler_params=params(),
        name=f"grads{head}",
    )(*pieces, *att, *grads, logs)


def load_rows(table, arrays, runs, rows_s, sems):
    for place, (which, row) in enumerate(runs):
        target = pl.multiple_of(table[place], 32)
        block = lax.shift_right_logical(table[place], 8)
        pltpu.make_async_copy(
            arrays[which].at[pl.ds(row, 32), :], rows_s.at[pl.ds(target, 32), :], sems.at[block]
        ).start()


def wait_rows(key, arrays, rows_s, sems):
    pltpu.make_async_copy(arrays[0], rows_s.at[pl.ds(key * PIECE, PIECE), :], sems.at[key]).wait()


def project_back_body(runs, table, own_ref, other_ref, *refs):
    arrays, refs = refs[:CTX], refs[CTX:]
    keep_ref, send_ref, rows_s, sems, grad_s = refs
    load_rows(table, arrays, runs, rows_s, sems)
    grad_s[0:ROWS, :] = own_ref[...]
    grad_s[ROWS:, :] = other_ref[...]
    for key in range(CTX):
        wait_rows(key, arrays, rows_s, sems)
        out = lax.dot_general(
            grad_s[...],
            rows_s[key * PIECE : (key + 1) * PIECE, :],
            (((1,), (1,)), ((), ())),
            preferred_element_type=f32,
        )
        keep_ref[key] = out[:ROWS]
        send_ref[key] = out[ROWS:].astype(bf16)


def project_back(runs, table, own, other, arrays):
    return pl.pallas_call(
        lambda *refs: project_back_body(runs, *refs),
        in_specs=[SMEM, VMEM, VMEM] + [ANY] * CTX,
        out_specs=[VMEM, VMEM],
        out_shape=[shape((CTX, ROWS, PIECE), f32), shape((CTX, ROWS, PIECE), bf16)],
        scratch_shapes=[
            pltpu.VMEM((HW, HALF), bf16),
            pltpu.SemaphoreType.DMA((CTX,)),
            pltpu.VMEM((2 * ROWS, HALF), bf16),
        ],
        compiler_params=params(),
        name="project_back",
    )(table, own, other, *arrays)


def project_body(runs, table, *refs):
    own, other, refs = refs[:CTX], refs[CTX], refs[CTX + 1 :]
    arrays, refs = refs[:CTX], refs[CTX:]
    keep_ref, send_ref, rows_s, sems, att_s, sum_s = refs
    load_rows(table, arrays, runs, rows_s, sems)
    for key in range(CTX):
        att_s[key, 0:ROWS, :] = own[key][...]
        att_s[key, ROWS:, :] = other[key]
    for key in range(CTX):
        wait_rows(key, arrays, rows_s, sems)
        part = jnp.dot(
            att_s[key],
            rows_s[key * PIECE : (key + 1) * PIECE, :],
            preferred_element_type=f32,
        )
        if key == 0:
            sum_s[...] = part
        else:
            sum_s[...] += part
    keep_ref[...] = sum_s[0:ROWS, :]
    send_ref[...] = sum_s[ROWS:, :].astype(bf16)


def project(runs, table, own, other, arrays):
    return pl.pallas_call(
        lambda *refs: project_body(runs, *refs),
        in_specs=[SMEM] + [VMEM] * (CTX + 1) + [ANY] * CTX,
        out_specs=[VMEM, VMEM],
        out_shape=[shape((ROWS, HALF), f32), shape((ROWS, HALF), bf16)],
        scratch_shapes=[
            pltpu.VMEM((HW, HALF), bf16),
            pltpu.SemaphoreType.DMA((CTX,)),
            pltpu.VMEM((CTX, 2 * ROWS, PIECE), bf16),
            pltpu.VMEM((2 * ROWS, HALF), f32),
        ],
        compiler_params=params(),
        name="project",
    )(table, *own, other, *arrays)


def join_body(keep_ref, got_ref, *outs):
    for key in range(CTX):
        outs[key][...] = (keep_ref[key] + got_ref[key].astype(f32)).astype(bf16)


def join(keep, got):
    return pl.pallas_call(
        join_body,
        in_specs=[VMEM, VMEM],
        out_specs=[VMEM] * CTX,
        out_shape=[shape((ROWS, PIECE), bf16)] * CTX,
        compiler_params=params(),
        name="join",
    )(keep, got)


COLS = 512
STEPS = HALF // COLS


def grad_proj_body(ids, *refs):
    ins, outs = refs[:8], refs[8:]
    for side in range(2):
        cot_ref, later_ref, gate_ref, conv_ref = ins[4 * side : 4 * side + 4]
        cot = cot_ref[...]
        ext = jnp.concatenate([cot, later_ref[...].astype(f32)], axis=0)
        grad = cot
        for offset in range(KSIZE):
            grad = grad + conv_ref[offset : offset + 1, :] * ext[offset * TOKF : offset * TOKF + ROWS]
        outs[side][...] = (gate_ref[...] * grad).astype(bf16)


def grad_proj(ids, cot, later, gate, conv):
    def spec(rows, side):
        return pl.BlockSpec((rows, COLS), lambda i, ids: (0, (ids[1] ^ side) * STEPS + i))

    ins = []
    for side in range(2):
        ins += [spec(ROWS, side), spec(SPAN, side), spec(1, side), spec(KSIZE, side)]
    return pl.pallas_call(
        grad_proj_body,
        grid_spec=pltpu.PrefetchScalarGridSpec(
            num_scalar_prefetch=1,
            grid=(STEPS,),
            in_specs=ins,
            out_specs=[pl.BlockSpec((ROWS, COLS), lambda i, ids: (0, i))] * 2,
        ),
        out_shape=[shape((ROWS, HALF), bf16)] * 2,
        compiler_params=params(),
        name="grad_proj",
    )(ids, *([cot, later, gate, conv] * 2))


def mix_body(ids, resid_ref, gate_ref, keep_ref, got_ref, mixed_ref, tail_ref):
    near = pl.program_id(0) < STEPS
    projected = jnp.where(near, keep_ref[...], got_ref[...].astype(f32))
    mixed = (resid_ref[...] + gate_ref[...] * projected).astype(bf16)
    mixed_ref[...] = mixed
    tail_ref[...] = mixed[ROWS - SPAN :]


def mix(ids, resid, gate, keep, got):
    def full(i, ids):
        return (0, (ids[1] ^ (i // STEPS)) * STEPS + i % STEPS)

    return pl.pallas_call(
        mix_body,
        grid_spec=pltpu.PrefetchScalarGridSpec(
            num_scalar_prefetch=1,
            grid=(2 * STEPS,),
            in_specs=[
                pl.BlockSpec((ROWS, COLS), full),
                pl.BlockSpec((1, COLS), full),
                pl.BlockSpec((ROWS, COLS), lambda i, ids: (0, jnp.minimum(i, STEPS - 1))),
                pl.BlockSpec((ROWS, COLS), lambda i, ids: (0, jnp.maximum(i, STEPS) - STEPS)),
            ],
            out_specs=[pl.BlockSpec((ROWS, COLS), full), pl.BlockSpec((SPAN, COLS), full)],
        ),
        out_shape=[shape((ROWS, D), bf16), shape((SPAN, D), bf16)],
        compiler_params=params(),
        name="mix",
    )(ids, resid, gate, keep, got)


def encode_body(mixed_ref, prior_ref, conv_ref, cot_ref, out_ref, sum_ref):
    mixed = mixed_ref[...].astype(f32)
    ext = jnp.concatenate([prior_ref[...].astype(f32), mixed], axis=0)
    cot = cot_ref[...]
    encoded = mixed
    sums = []
    for offset in range(KSIZE):
        begin = SPAN - offset * TOKF
        earlier = ext[begin : begin + ROWS]
        encoded = encoded + conv_ref[offset : offset + 1, :] * earlier
        sums.append(jnp.sum(cot * earlier, axis=0, keepdims=True))
    out_ref[...] = encoded
    sum_ref[...] = jnp.concatenate(sums, axis=0)


def encode(mixed, prior, conv, cot):
    def spec(rows):
        return pl.BlockSpec((rows, COLS), lambda i: (0, i))

    return pl.pallas_call(
        encode_body,
        grid=(D // COLS,),
        in_specs=[spec(ROWS), spec(SPAN), spec(KSIZE), spec(ROWS)],
        out_specs=[spec(ROWS), spec(KSIZE)],
        out_shape=[shape((ROWS, D), f32), shape((KSIZE, D), f32)],
        compiler_params=params(),
        name="encode",
    )(mixed, prior, conv, cot)


def unpack_body(ids, *refs):
    firsts, seconds, outs = refs[:CTX], refs[CTX : 2 * CTX], refs[2 * CTX :]
    for key in range(CTX):
        for head, group in enumerate((firsts, seconds)):
            start = pl.multiple_of((ids[0] ^ key) * PIECE + head * HDIM, HDIM)
            for place in range(3):
                outs[place][:, pl.ds(start, HDIM)] = group[key][
                    :, place * HDIM : (place + 1) * HDIM
                ]


def unpack(ids, firsts, seconds):
    return pl.pallas_call(
        unpack_body,
        in_specs=[SMEM] + [VMEM] * (2 * CTX),
        out_specs=[VMEM] * 3,
        out_shape=[shape((ROWS, HW), bf16)] * 3,
        compiler_params=params(),
        name="unpack",
    )(ids, *firsts, *seconds)


def exchange(pieces):
    return [pieces[0]] + [swap(pieces[key], "ctx", key) for key in range(1, CTX)]


def tree_sum(parts):
    while len(parts) > 1:
        parts = [parts[i] + parts[i + 1] for i in range(0, len(parts), 2)]
    return parts[0]


def sum_over(value, axis, masks):
    return tree_sum([value] + [swap(value, axis, mask) for mask in masks])


def shards(queries, keys, values, resid, gate, out_weight, conv_weight, cotangent):
    ctx = lax.axis_index("ctx")
    fsdp = lax.axis_index("fsdp")
    core = fsdp % 2
    ids = jnp.stack([ctx, core]).astype(jnp.int32)

    other_rows = shift(out_weight, "core", 1)
    mine = lax.dynamic_slice(out_weight, (0, core * HALF), (16, HALF))
    theirs = lax.dynamic_slice(other_rows, (0, core * HALF), (16, HALF))
    rows = jnp.where(
        core == 0,
        jnp.concatenate([mine, theirs], axis=0),
        jnp.concatenate([theirs, mine], axis=0),
    )
    gathered = gather_rows(rows)
    arrays = [g[0] for g in gathered]
    runs = []
    for which, (_, offs) in enumerate(gathered):
        for place, off in enumerate(offs):
            runs.append((off["z"] % 4, off["x"] % 2, which, place * 32, off))
    runs.sort(key=lambda run: run[:4])
    dx, dy, dz = (np.array([run[4][d] for run in runs], np.int32) for d in "xyz")
    x_lo, z = ctx // 4, ctx % 4
    x = (fsdp // 2 % 2) * 2 + x_lo
    run_x = (x + dx) % 4
    run_y = (fsdp // 4 + dy) % 4
    run_z = (z + dz) % 4
    block = ((run_x % 2) ^ x_lo) * 4 + (run_z ^ z)
    table = (block * PIECE + run_y * 64 + (run_x // 2) * 32).astype(jnp.int32)
    runs = [run[2:4] for run in runs]

    pieces = exchange(pack(ids, queries[0], keys[0], values[0]))
    later = along(cotangent[0, :SPAN].astype(bf16), -1)
    own_grad, send_grad = grad_proj(ids, cotangent[0], later, gate, conv_weight)
    other_grad = shift(send_grad, "core", 1)

    results = forward(pieces)
    att, logs = results[:CTX], results[CTX]
    own_att = exchange(att)
    other_att = shift(jnp.stack(own_att), "core", 1)

    keep, send = project_back(runs, table, own_grad, other_grad, arrays)
    grads = exchange(join(keep, shift(send, "core", 1)))

    keep, send = project(runs, table, own_att, other_att, arrays)
    mixed, tail = mix(ids, resid[0], gate, keep, shift(send, "core", 1))
    prior = along(tail, 1)
    encoded, sums = encode(mixed, prior, conv_weight, cotangent[0])
    sums = sum_over(sums, "ctx", range(1, 8))
    sums = sum_over(sums, "fsdp", (4, 8, 12))
    grad_conv = sum_over(sums, "fsdp", (1, 2, 3))

    firsts = exchange(backward(0, pieces, att, grads, logs))
    seconds = exchange(backward(1, pieces, att, grads, logs))
    grad_q, grad_k, grad_v = unpack(ids, firsts, seconds)
    return (encoded[None], grad_q[None], grad_k[None], grad_v[None], grad_conv)


def solution(mesh):
    token = P("fsdp", "ctx", None)
    in_specs = (
        token,
        token,
        token,
        token,
        P("fsdp", None),
        P(("ctx", "fsdp"), None),
        P(),
        token,
    )
    return jax.shard_map(
        shards,
        mesh=mesh,
        in_specs=in_specs,
        out_specs=(token, token, token, token, P()),
        check_vma=False,
    )
```

```python
import math

import jax
import jax.numpy as jnp
import numpy as np
from jax import lax
from jax.experimental import pallas as pl
from jax.experimental.pallas import tpu as pltpu
from jax.sharding import PartitionSpec as P


HDIM = 128
KSIZE = 3
TOKF = 48
CTX = 8
PARTS = 12
ROWS = 192
SEQ = CTX * ROWS
HW = 2048
D = 4096
HALF = D // 2
SPAN = (KSIZE - 1) * TOKF
PIECE = HW // CTX
BLOCK = 256
FACTOR = 1.0 / math.sqrt(HDIM)
LOG2E = math.log2(math.e)
AXES = ("ctx", "fsdp")
bf16 = jnp.bfloat16
f32 = jnp.float32


def coords(flat):
    ctx, fsdp = divmod(flat, 16)
    x_lo, z = divmod(ctx, 4)
    y, rest = divmod(fsdp, 4)
    x_hi, core = divmod(rest, 2)
    return dict(x=x_hi * 2 + x_lo, y=y, z=z, core=core)


def flat_of(place):
    x_hi, x_lo = divmod(place["x"], 2)
    return (x_lo * 4 + place["z"]) * 16 + place["y"] * 4 + x_hi * 2 + place["core"]


def shift(array, dim, by):
    size = 2 if dim == "core" else 4
    pairs = []
    for source in range(128):
        place = coords(source)
        place[dim] = (place[dim] + by) % size
        pairs.append((source, flat_of(place)))
    return lax.ppermute(array, AXES, pairs)


def swap(array, axis, key):
    count = lax.axis_size(axis)
    return lax.ppermute(array, axis, [(i, i ^ key) for i in range(count)])


def along(array, by):
    pairs = [(i, i + by) for i in range(CTX) if 0 <= i + by < CTX]
    return lax.ppermute(array, "ctx", pairs)


def moved(offsets, dim, by):
    return [dict(o, **{dim: o[dim] - by}) for o in offsets]


def gather_rows(rows):
    got = [(rows, [dict(x=0, y=0, z=0)])]
    for by in (1, -1, 2):
        got.append((shift(rows, "z", by), moved(got[0][1], "z", by)))
    plane = jnp.concatenate([g[0] for g in got], axis=0)
    offs = [o for g in got for o in g[1]]
    got = [(plane, offs)]
    for by in (1, -1, 2):
        got.append((shift(plane, "x", by), moved(offs, "x", by)))
    far = jnp.concatenate([got[2][0], got[3][0]], axis=0)
    got = got[:2] + [(far, got[2][1] + got[3][1])]
    ups, downs, out = {}, {}, list(got)
    ups[0] = shift(plane, "y", 1)
    downs[0] = shift(plane, "y", -1)
    for up, down in ((1, 2), (2, 1)):
        ups[up] = shift(got[up][0], "y", 1)
        downs[down] = shift(got[down][0], "y", -1)
    twice = [shift(ups[0], "y", 1), shift(ups[1], "y", 1), shift(downs[2], "y", -1)]
    for place in range(3):
        out.append((ups[place], moved(got[place][1], "y", 1)))
        out.append((downs[place], moved(got[place][1], "y", -1)))
        out.append((twice[place], moved(got[place][1], "y", 2)))
    return out


def params(mib=56):
    return pltpu.CompilerParams(vmem_limit_bytes=mib * 2**20)


SMEM = pl.BlockSpec(memory_space=pltpu.SMEM)
VMEM = pl.BlockSpec(memory_space=pltpu.VMEM)
ANY = pl.BlockSpec(memory_space=pl.ANY)


def shape(dims, dtype):
    return jax.ShapeDtypeStruct(dims, dtype)


def pack_body(ids, q_ref, k_ref, v_ref, *outs):
    for key in range(CTX):
        start = pl.multiple_of((ids[0] ^ key) * PIECE, PIECE)
        for place, ref in enumerate((q_ref, k_ref, v_ref)):
            outs[key][:, place * PIECE : (place + 1) * PIECE] = ref[:, pl.ds(start, PIECE)]


def pack(ids, queries, keys, values):
    return pl.pallas_call(
        pack_body,
        in_specs=[SMEM, VMEM, VMEM, VMEM],
        out_specs=[VMEM] * CTX,
        out_shape=[shape((ROWS, 3 * PIECE), bf16)] * CTX,
        compiler_params=params(10),
        name="pack",
    )(ids, queries, keys, values)


def forward_body(*refs):
    pieces, refs = refs[:CTX], refs[CTX:]
    outs, refs = refs[:CTX], refs[CTX:]
    log_ref, q_s, k_s, v_s, o_s = refs
    for head in range(2):
        for key in range(CTX):
            rows = slice(key * ROWS, (key + 1) * ROWS)
            for place, ref in enumerate((q_s, k_s, v_s)):
                start = place * PIECE + head * HDIM
                ref[head, rows, :] = pieces[key][:, start : start + HDIM]

    def step(index, carry):
        head = index // (SEQ // BLOCK)
        start = pl.multiple_of((index % (SEQ // BLOCK)) * BLOCK, BLOCK)
        query = q_s[head, pl.ds(start, BLOCK), :]
        scores = lax.dot_general(
            query, k_s[head], (((1,), (1,)), ((), ())), preferred_element_type=f32
        )
        peak = jnp.max(scores, axis=1, keepdims=True)
        raised = jnp.exp2((scores - peak) * (FACTOR * LOG2E))
        totals = jnp.sum(raised, axis=1, keepdims=True)
        summed = jnp.dot(raised.astype(bf16), v_s[head], preferred_element_type=f32)
        o_s[head, pl.ds(start, BLOCK), :] = (summed / totals).astype(bf16)
        logs = peak * (FACTOR * LOG2E) + jnp.log2(totals)
        log_ref[head, :, pl.ds(start, BLOCK)] = jnp.broadcast_to(logs, (BLOCK, HDIM)).T[:8]
        return carry

    lax.fori_loop(0, 2 * SEQ // BLOCK, step, 0)
    for key in range(CTX):
        rows = slice(key * ROWS, (key + 1) * ROWS)
        outs[key][:, :HDIM] = o_s[0, rows, :]
        outs[key][:, HDIM:] = o_s[1, rows, :]


def forward(pieces):
    return pl.pallas_call(
        forward_body,
        in_specs=[VMEM] * CTX,
        out_specs=[VMEM] * (CTX + 1),
        out_shape=[shape((ROWS, PIECE), bf16)] * CTX + [shape((2, 8, SEQ), f32)],
        scratch_shapes=[pltpu.VMEM((2, SEQ, HDIM), bf16)] * 4,
        compiler_params=params(24),
        name="attend",
    )(*pieces)


def backward_body(head, *refs):
    pieces, refs = refs[:CTX], refs[CTX:]
    att, refs = refs[:CTX], refs[CTX:]
    grads, refs = refs[:CTX], refs[CTX:]
    log_ref, refs = refs[0], refs[1:]
    outs, refs = refs[:CTX], refs[CTX:]
    q_s, k_s, v_s, g_s, d_s, kt_s, dq_s, dk_s, dv_s = refs
    cols = slice(head * HDIM, (head + 1) * HDIM)
    for key in range(CTX):
        rows = slice(key * ROWS, (key + 1) * ROWS)
        for place, ref in enumerate((q_s, k_s, v_s)):
            start = place * PIECE + head * HDIM
            ref[rows, :] = pieces[key][:, start : start + HDIM]
        grad = grads[key][:, cols]
        g_s[rows, :] = grad
        d_s[rows, :] = grad.astype(f32) * att[key][:, cols].astype(f32)
    kt_s[...] = k_s[...].astype(f32).T.astype(bf16)
    dk_s[...] = jnp.zeros_like(dk_s)
    dv_s[...] = jnp.zeros_like(dv_s)
    wide = 512

    def step(index, carry):
        start = pl.multiple_of(index * BLOCK, BLOCK)
        query = q_s[pl.ds(start, BLOCK), :]
        grad = g_s[pl.ds(start, BLOCK), :]
        delta = jnp.sum(d_s[pl.ds(start, BLOCK), :].T, axis=0, keepdims=True)
        logs = log_ref[head, 0:1, pl.ds(start, BLOCK)]
        dq = jnp.zeros((HDIM, BLOCK), f32)
        for chunk in range(SEQ // wide):
            part = slice(chunk * wide, (chunk + 1) * wide)
            scores = lax.dot_general(
                k_s[part, :], query, (((1,), (1,)), ((), ())), preferred_element_type=f32
            )
            dprob = lax.dot_general(
                v_s[part, :], grad, (((1,), (1,)), ((), ())), preferred_element_type=f32
            )
            probs = jnp.exp2(scores * (FACTOR * LOG2E) - logs)
            dscore = (probs * (dprob - delta)).astype(bf16)
            dv_s[part, :] += jnp.dot(probs.astype(bf16), grad, preferred_element_type=f32)
            dk_s[part, :] += jnp.dot(dscore, query, preferred_element_type=f32)
            dq = dq + jnp.dot(kt_s[:, part], dscore, preferred_element_type=f32)
        dq_s[pl.ds(start, BLOCK), :] = (dq.T * FACTOR).astype(bf16)
        return carry

    lax.fori_loop(0, SEQ // BLOCK, step, 0)
    for key in range(CTX):
        rows = slice(key * ROWS, (key + 1) * ROWS)
        outs[key][:, :HDIM] = dq_s[rows, :]
        outs[key][:, HDIM : 2 * HDIM] = (dk_s[rows, :] * FACTOR).astype(bf16)
        outs[key][:, 2 * HDIM :] = dv_s[rows, :].astype(bf16)


def backward(head, pieces, att, grads, logs):
    return pl.pallas_call(
        lambda *refs: backward_body(head, *refs),
        in_specs=[VMEM] * (3 * CTX + 1),
        out_specs=[VMEM] * CTX,
        out_shape=[shape((ROWS, 3 * HDIM), bf16)] * CTX,
        scratch_shapes=[pltpu.VMEM((SEQ, HDIM), bf16)] * 4
        + [
            pltpu.VMEM((SEQ, HDIM), f32),
            pltpu.VMEM((HDIM, SEQ), bf16),
            pltpu.VMEM((SEQ, HDIM), bf16),
            pltpu.VMEM((SEQ, HDIM), f32),
            pltpu.VMEM((SEQ, HDIM), f32),
        ],
        compiler_params=params(24),
    )(*pieces, *att, *grads, logs)


def load_rows(table, arrays, runs, rows_s, sems):
    for place, (which, row) in enumerate(runs):
        target = pl.multiple_of(table[place], 32)
        block = lax.shift_right_logical(table[place], 8)
        pltpu.make_async_copy(
            arrays[which].at[pl.ds(row, 32), :], rows_s.at[pl.ds(target, 32), :], sems.at[block]
        ).start()


def wait_rows(key, rows_s, sems):
    rows = rows_s.at[pl.ds(pl.multiple_of(key * PIECE, PIECE), PIECE), :]
    pltpu.make_async_copy(rows, rows, sems.at[key]).wait()


def project_back_body(runs, table, own_ref, other_ref, *refs):
    arrays, refs = refs[:PARTS], refs[PARTS:]
    keep_ref, send_ref, rows_s, sems, grad_s = refs
    load_rows(table, arrays, runs, rows_s, sems)
    grad_s[0:ROWS, :] = own_ref[...]
    grad_s[ROWS:, :] = other_ref[...]

    def step(key, carry):
        wait_rows(key, rows_s, sems)
        out = lax.dot_general(
            grad_s[...],
            rows_s[pl.ds(pl.multiple_of(key * PIECE, PIECE), PIECE), :],
            (((1,), (1,)), ((), ())),
            preferred_element_type=f32,
        )
        keep_ref[key] = out[:ROWS]
        send_ref[key] = out[ROWS:].astype(bf16)
        return carry

    lax.fori_loop(0, CTX, step, 0)


def project_back(runs, table, own, other, arrays):
    return pl.pallas_call(
        lambda *refs: project_back_body(runs, *refs),
        in_specs=[SMEM, VMEM, VMEM] + [ANY] * PARTS,
        out_specs=[VMEM, VMEM],
        out_shape=[shape((CTX, ROWS, PIECE), f32), shape((CTX, ROWS, PIECE), bf16)],
        scratch_shapes=[
            pltpu.VMEM((HW, HALF), bf16),
            pltpu.SemaphoreType.DMA((CTX,)),
            pltpu.VMEM((2 * ROWS, HALF), bf16),
        ],
        compiler_params=params(32),
        name="project_back",
    )(table, own, other, *arrays)


def project_body(runs, table, *refs):
    own, other, refs = refs[0], refs[1], refs[2:]
    arrays, refs = refs[:PARTS], refs[PARTS:]
    keep_ref, send_ref, rows_s, sems, att_s, sum_s = refs
    load_rows(table, arrays, runs, rows_s, sems)
    for key in range(CTX):
        att_s[key, 0:ROWS, :] = own[key]
        att_s[key, ROWS:, :] = other[key]
    sum_s[...] = jnp.zeros_like(sum_s)

    def step(key, carry):
        wait_rows(key, rows_s, sems)
        sum_s[...] += jnp.dot(
            att_s[key],
            rows_s[pl.ds(pl.multiple_of(key * PIECE, PIECE), PIECE), :],
            preferred_element_type=f32,
        )
        return carry

    lax.fori_loop(0, CTX, step, 0)
    keep_ref[...] = sum_s[0:ROWS, :]
    send_ref[...] = sum_s[ROWS:, :].astype(bf16)


def project(runs, table, own, other, arrays):
    return pl.pallas_call(
        lambda *refs: project_body(runs, *refs),
        in_specs=[SMEM] + [VMEM] * 2 + [ANY] * PARTS,
        out_specs=[VMEM, VMEM],
        out_shape=[shape((ROWS, HALF), f32), shape((ROWS, HALF), bf16)],
        scratch_shapes=[
            pltpu.VMEM((HW, HALF), bf16),
            pltpu.SemaphoreType.DMA((CTX,)),
            pltpu.VMEM((CTX, 2 * ROWS, PIECE), bf16),
            pltpu.VMEM((2 * ROWS, HALF), f32),
        ],
        compiler_params=params(32),
        name="project",
    )(table, own, other, *arrays)


def stack_body(*refs):
    for key in range(CTX):
        refs[CTX][key] = refs[key][...]


def stack(pieces):
    return pl.pallas_call(
        stack_body,
        in_specs=[VMEM] * CTX,
        out_specs=VMEM,
        out_shape=shape((CTX, ROWS, PIECE), bf16),
        compiler_params=params(10),
        name="stack",
    )(*pieces)


def join_body(keep_ref, got_ref, *outs):
    for key in range(CTX):
        outs[key][...] = (keep_ref[key] + got_ref[key].astype(f32)).astype(bf16)


def join(keep, got):
    return pl.pallas_call(
        join_body,
        in_specs=[VMEM, VMEM],
        out_specs=[VMEM] * CTX,
        out_shape=[shape((ROWS, PIECE), bf16)] * CTX,
        compiler_params=params(10),
        name="join",
    )(keep, got)


COLS = 512
STEPS = HALF // COLS


def grad_proj_body(ids, *refs):
    ins, outs = refs[:8], refs[8:]
    for side in range(2):
        cot_ref, later_ref, gate_ref, conv_ref = ins[4 * side : 4 * side + 4]
        cot = cot_ref[...]
        ext = jnp.concatenate([cot, later_ref[...].astype(f32)], axis=0)
        grad = cot
        for offset in range(KSIZE):
            grad = grad + conv_ref[offset : offset + 1, :] * ext[offset * TOKF : offset * TOKF + ROWS]
        outs[side][...] = (gate_ref[...] * grad).astype(bf16)


def grad_proj(ids, cot, later, gate, conv):
    def spec(rows, side):
        return pl.BlockSpec((rows, COLS), lambda i, ids: (0, (ids[1] ^ side) * STEPS + i))

    ins = []
    for side in range(2):
        ins += [spec(ROWS, side), spec(SPAN, side), spec(1, side), spec(KSIZE, side)]
    return pl.pallas_call(
        grad_proj_body,
        grid_spec=pltpu.PrefetchScalarGridSpec(
            num_scalar_prefetch=1,
            grid=(STEPS,),
            in_specs=ins,
            out_specs=[pl.BlockSpec((ROWS, COLS), lambda i, ids: (0, i))] * 2,
        ),
        out_shape=[shape((ROWS, HALF), bf16)] * 2,
        compiler_params=params(16),
        name="grad_proj",
    )(ids, *([cot, later, gate, conv] * 2))


def mix_body(ids, resid_ref, gate_ref, keep_ref, got_ref, mixed_ref, tail_ref):
    near = pl.program_id(0) < STEPS
    projected = jnp.where(near, keep_ref[...], got_ref[...].astype(f32))
    mixed = (resid_ref[...] + gate_ref[...] * projected).astype(bf16)
    mixed_ref[...] = mixed
    tail_ref[...] = mixed[ROWS - SPAN :]


def mix(ids, resid, gate, keep, got):
    def full(i, ids):
        return (0, (ids[1] ^ (i // STEPS)) * STEPS + i % STEPS)

    return pl.pallas_call(
        mix_body,
        grid_spec=pltpu.PrefetchScalarGridSpec(
            num_scalar_prefetch=1,
            grid=(2 * STEPS,),
            in_specs=[
                pl.BlockSpec((ROWS, COLS), full),
                pl.BlockSpec((1, COLS), full),
                pl.BlockSpec((ROWS, COLS), lambda i, ids: (0, jnp.minimum(i, STEPS - 1))),
                pl.BlockSpec((ROWS, COLS), lambda i, ids: (0, jnp.maximum(i, STEPS) - STEPS)),
            ],
            out_specs=[pl.BlockSpec((ROWS, COLS), full), pl.BlockSpec((SPAN, COLS), full)],
        ),
        out_shape=[shape((ROWS, D), bf16), shape((SPAN, D), bf16)],
        compiler_params=params(16),
        name="mix",
    )(ids, resid, gate, keep, got)


def encode_body(mixed_ref, prior_ref, conv_ref, cot_ref, out_ref, sum_ref):
    mixed = mixed_ref[...].astype(f32)
    ext = jnp.concatenate([prior_ref[...].astype(f32), mixed], axis=0)
    cot = cot_ref[...]
    encoded = mixed
    for offset in range(KSIZE):
        begin = SPAN - offset * TOKF
        earlier = ext[begin : begin + ROWS]
        encoded = encoded + conv_ref[offset : offset + 1, :] * earlier
        row = offset * (D // COLS) + pl.program_id(0)
        sum_ref[pl.ds(row, 1), :] = jnp.sum(cot * earlier, axis=0, keepdims=True)
    out_ref[...] = encoded


def encode(mixed, prior, conv, cot):
    def spec(rows):
        return pl.BlockSpec((rows, COLS), lambda i: (0, i))

    return pl.pallas_call(
        encode_body,
        grid=(D // COLS,),
        in_specs=[spec(ROWS), spec(SPAN), spec(KSIZE), spec(ROWS)],
        out_specs=[spec(ROWS), pl.BlockSpec((KSIZE * D // COLS, COLS), lambda i: (0, 0))],
        out_shape=[shape((ROWS, D), f32), shape((KSIZE * D // COLS, COLS), f32)],
        compiler_params=params(16),
        name="encode",
    )(mixed, prior, conv, cot)


def unpack_body(ids, *refs):
    groups, outs = (refs[:CTX], refs[CTX : 2 * CTX]), refs[2 * CTX :]
    for key in range(CTX):
        for head, group in enumerate(groups):
            start = pl.multiple_of((ids[0] ^ key) * PIECE + head * HDIM, HDIM)
            for place in range(3):
                part = slice(place * HDIM, (place + 1) * HDIM)
                outs[place][:, pl.ds(start, HDIM)] = group[key][:, part]


def unpack(ids, firsts, seconds):
    return pl.pallas_call(
        unpack_body,
        in_specs=[SMEM] + [VMEM] * (2 * CTX),
        out_specs=[VMEM] * 3,
        out_shape=[shape((ROWS, HW), bf16)] * 3,
        compiler_params=params(12),
        name="unpack",
    )(ids, *firsts, *seconds)


def exchange(pieces, keys=range(1, CTX)):
    got = [swap(pieces[key], "ctx", key) for key in keys]
    return got if keys[0] > 1 else [pieces[0]] + got


def exchange_in(pieces, groups):
    got = []
    for keys in groups:
        got += exchange(pieces, range(*keys))
    return got


def after(values, *others):
    return lax.optimization_barrier((values, others))[0]


def add_swap(sums, axis, mask):
    return sums + swap(sums, axis, mask)


def block(queries, keys, values, resid, gate, out_weight, conv_weight, cotangent):
    ctx = lax.axis_index("ctx")
    fsdp = lax.axis_index("fsdp")
    core = fsdp % 2
    ids = jnp.stack([ctx, core]).astype(jnp.int32)

    other_rows = shift(out_weight, "core", 1)
    mine = lax.dynamic_slice(out_weight, (0, core * HALF), (16, HALF))
    theirs = lax.dynamic_slice(other_rows, (0, core * HALF), (16, HALF))
    rows = jnp.where(
        core == 0,
        jnp.concatenate([mine, theirs], axis=0),
        jnp.concatenate([theirs, mine], axis=0),
    )
    gathered = gather_rows(rows)
    arrays = [g[0] for g in gathered]
    runs = []
    for which, (_, offs) in enumerate(gathered):
        for place, off in enumerate(offs):
            runs.append((off["z"] % 4, off["x"] % 2, which, place * 32, off))
    runs.sort(key=lambda run: run[:4])
    dx, dy, dz = (np.array([run[4][d] for run in runs], np.int32) for d in "xyz")
    x_lo, z = ctx // 4, ctx % 4
    x = (fsdp // 2 % 2) * 2 + x_lo
    run_x = (x + dx) % 4
    run_y = (fsdp // 4 + dy) % 4
    run_z = (z + dz) % 4
    block = ((run_x % 2) ^ x_lo) * 4 + (run_z ^ z)
    table = (block * PIECE + run_y * 64 + (run_x // 2) * 32).astype(jnp.int32)
    runs = [run[2:4] for run in runs]

    packed = pack(ids, queries[0], keys[0], values[0])
    pieces = exchange(packed, range(1, 4))
    pieces += exchange(packed, range(4, CTX))
    later = along(cotangent[0, :SPAN].astype(bf16), -1)
    results = forward(after(pieces, arrays[0], arrays[1]))
    att, logs = results[:CTX], results[CTX]
    own_att = exchange(att)
    own_grad, send_grad = grad_proj(ids, cotangent[0], later, gate, conv_weight)
    other_grad = shift(send_grad, "core", 1)
    keep, send = project_back(runs, table, own_grad, other_grad, arrays)
    got = shift(send, "core", 1)
    own_att = stack(own_att)
    other_att = shift(own_att, "core", 1)
    joined = join(keep, got)
    grads = exchange(joined)

    keep, send = project(runs, table, after(own_att, joined[0]), other_att, arrays)
    mixed, tail = mix(ids, resid[0], gate, keep, shift(send, "core", 1))
    prior = along(tail, 1)

    firsts = backward(0, pieces, att, after(grads, tail), logs)
    encoded, sums = encode(mixed, prior, conv_weight, after(cotangent[0], firsts[0]))
    sums = add_swap(sums, "fsdp", 1)
    early = exchange_in(firsts, ((1, 4), (4, 8)))
    sums = add_swap(sums, "fsdp", 4)
    sums = add_swap(sums, "fsdp", 8)
    seconds = backward(1, pieces, att, grads, logs)
    sums = add_swap(after(sums, seconds[0]), "fsdp", 2)
    late = exchange_in(seconds, ((1, 3), (3, 6), (6, 8)))
    sums = add_swap(sums, "ctx", 4)
    sums = add_swap(sums, "ctx", 1)
    sums = add_swap(sums, "ctx", 2)
    grad_conv = sums.reshape(KSIZE, D)
    grad_q, grad_k, grad_v = unpack(ids, early, late)
    return (encoded[None], grad_q[None], grad_k[None], grad_v[None], grad_conv)


def solution(mesh):
    token = P("fsdp", "ctx", None)
    in_specs = (
        token,
        token,
        token,
        token,
        P("fsdp", None),
        P(("ctx", "fsdp"), None),
        P(),
        token,
    )
    return jax.shard_map(
        block,
        mesh=mesh,
        in_specs=in_specs,
        out_specs=(token, token, token, token, P()),
        check_vma=False,
    )
```

```python
import math

import jax
import jax.numpy as jnp
import numpy as np
from jax import lax
from jax.experimental import pallas as pl
from jax.experimental.pallas import tpu as pltpu
from jax.sharding import PartitionSpec as P


HDIM = 128
KSIZE = 3
TOKF = 48
CTX = 8
PARTS = 12
ROWS = 192
SEQ = CTX * ROWS
HW = 2048
D = 4096
HALF = D // 2
SPAN = (KSIZE - 1) * TOKF
PIECE = HW // CTX
BLOCK = 256
WIDE = 512
FACTOR = 1.0 / math.sqrt(HDIM)
LOG2E = math.log2(math.e)
AXES = ("ctx", "fsdp")
bf16 = jnp.bfloat16
f32 = jnp.float32


def coords(flat):
    ctx, fsdp = divmod(flat, 16)
    x_lo, z = divmod(ctx, 4)
    y, rest = divmod(fsdp, 4)
    x_hi, core = divmod(rest, 2)
    return dict(x=x_hi * 2 + x_lo, y=y, z=z, core=core)


def flat_of(place):
    x_hi, x_lo = divmod(place["x"], 2)
    return (x_lo * 4 + place["z"]) * 16 + place["y"] * 4 + x_hi * 2 + place["core"]


def shift(array, dim, by):
    size = 2 if dim == "core" else 4
    pairs = []
    for source in range(128):
        place = coords(source)
        place[dim] = (place[dim] + by) % size
        pairs.append((source, flat_of(place)))
    return lax.ppermute(array, AXES, pairs)


def swap(array, axis, key):
    count = lax.axis_size(axis)
    return lax.ppermute(array, axis, [(i, i ^ key) for i in range(count)])


def along(array, by):
    pairs = [(i, i + by) for i in range(CTX) if 0 <= i + by < CTX]
    return lax.ppermute(array, "ctx", pairs)


def moved(offsets, dim, by):
    return [dict(o, **{dim: o[dim] - by}) for o in offsets]


def gather_rows(rows):
    got = [(rows, [dict(x=0, y=0, z=0)])]
    for by in (1, -1, 2):
        got.append((shift(rows, "z", by), moved(got[0][1], "z", by)))
    plane = jnp.concatenate([g[0] for g in got], axis=0)
    offs = [o for g in got for o in g[1]]
    got = [(plane, offs)]
    for by in (1, -1, 2):
        got.append((shift(plane, "x", by), moved(offs, "x", by)))
    far = jnp.concatenate([got[2][0], got[3][0]], axis=0)
    got = got[:2] + [(far, got[2][1] + got[3][1])]
    ups, downs, out = {}, {}, list(got)
    ups[0] = shift(plane, "y", 1)
    downs[0] = shift(plane, "y", -1)
    twice = [shift(ups[0], "y", 1)]
    for up, down in ((1, 2), (2, 1)):
        ups[up] = shift(got[up][0], "y", 1)
        downs[down] = shift(got[down][0], "y", -1)
    twice += [shift(ups[1], "y", 1), shift(downs[2], "y", -1)]
    for place in range(3):
        out.append((ups[place], moved(got[place][1], "y", 1)))
        out.append((downs[place], moved(got[place][1], "y", -1)))
        out.append((twice[place], moved(got[place][1], "y", 2)))
    return out


def params(mib=56):
    return pltpu.CompilerParams(vmem_limit_bytes=mib * 2**20)


SMEM = pl.BlockSpec(memory_space=pltpu.SMEM)
VMEM = pl.BlockSpec(memory_space=pltpu.VMEM)
ANY = pl.BlockSpec(memory_space=pl.ANY)


def shape(dims, dtype):
    return jax.ShapeDtypeStruct(dims, dtype)


def pack_body(ids, q_ref, k_ref, v_ref, *outs):
    for key in range(CTX):
        start = pl.multiple_of((ids[0] ^ key) * PIECE, PIECE)
        for place, ref in enumerate((q_ref, k_ref, v_ref)):
            outs[key][:, place * PIECE : (place + 1) * PIECE] = ref[:, pl.ds(start, PIECE)]


def pack(ids, queries, keys, values):
    return pl.pallas_call(
        pack_body,
        in_specs=[SMEM, VMEM, VMEM, VMEM],
        out_specs=[VMEM] * CTX,
        out_shape=[shape((ROWS, 3 * PIECE), bf16)] * CTX,
        compiler_params=params(),
        name="pack",
    )(ids, queries, keys, values)


def forward_body(*refs):
    pieces, refs = refs[:CTX], refs[CTX:]
    outs, refs = refs[:CTX], refs[CTX:]
    log_ref, q_s, k_s, v_s, o_s = refs
    for head in range(2):
        for key in range(CTX):
            rows = slice(key * ROWS, (key + 1) * ROWS)
            for place, ref in enumerate((q_s, k_s, v_s)):
                start = place * PIECE + head * HDIM
                ref[head, rows, :] = pieces[key][:, start : start + HDIM]

    def step(index, carry):
        head = index // (SEQ // BLOCK)
        start = pl.multiple_of((index % (SEQ // BLOCK)) * BLOCK, BLOCK)
        query = q_s[head, pl.ds(start, BLOCK), :]
        scores = lax.dot_general(
            query, k_s[head], (((1,), (1,)), ((), ())), preferred_element_type=f32
        )
        peak = jnp.max(scores, axis=1, keepdims=True)
        raised = jnp.exp2((scores - peak) * (FACTOR * LOG2E))
        totals = jnp.sum(raised, axis=1, keepdims=True)
        summed = jnp.dot(raised.astype(bf16), v_s[head], preferred_element_type=f32)
        o_s[head, pl.ds(start, BLOCK), :] = (summed / totals).astype(bf16)
        logs = peak * (FACTOR * LOG2E) + jnp.log2(totals)
        log_ref[head, :, pl.ds(start, BLOCK)] = jnp.broadcast_to(logs, (BLOCK, HDIM)).T[:8]
        return carry

    lax.fori_loop(0, 2 * SEQ // BLOCK, step, 0)
    for key in range(CTX):
        rows = slice(key * ROWS, (key + 1) * ROWS)
        outs[key][:, :HDIM] = o_s[0, rows, :]
        outs[key][:, HDIM:] = o_s[1, rows, :]


def forward(pieces):
    return pl.pallas_call(
        forward_body,
        in_specs=[VMEM] * CTX,
        out_specs=[VMEM] * (CTX + 1),
        out_shape=[shape((ROWS, PIECE), bf16)] * CTX + [shape((2, 8, SEQ), f32)],
        scratch_shapes=[pltpu.VMEM((2, SEQ, HDIM), bf16)] * 4,
        compiler_params=params(20),
        name="attend",
    )(*pieces)


def backward_body(head, *refs):
    pieces, refs = refs[:CTX], refs[CTX:]
    att, refs = refs[:CTX], refs[CTX:]
    grads, refs = refs[:CTX], refs[CTX:]
    log_ref, refs = refs[0], refs[1:]
    outs, refs = refs[:CTX], refs[CTX:]
    q_s, k_s, v_s, g_s, d_s, kt_s, dq_s, dk_s, dv_s = refs
    cols = slice(head * HDIM, (head + 1) * HDIM)
    for key in range(CTX):
        rows = slice(key * ROWS, (key + 1) * ROWS)
        for place, ref in enumerate((q_s, k_s, v_s)):
            start = place * PIECE + head * HDIM
            ref[rows, :] = pieces[key][:, start : start + HDIM]
        grad = grads[key][:, cols]
        g_s[rows, :] = grad
        d_s[rows, :] = grad.astype(f32) * att[key][:, cols].astype(f32)
    kt_s[...] = k_s[...].astype(f32).T.astype(bf16)
    dk_s[...] = jnp.zeros_like(dk_s)
    dv_s[...] = jnp.zeros_like(dv_s)

    def step(index, carry):
        start = pl.multiple_of(index * WIDE, WIDE)
        query = q_s[pl.ds(start, WIDE), :]
        grad = g_s[pl.ds(start, WIDE), :]
        delta = jnp.sum(d_s[pl.ds(start, WIDE), :].T, axis=0, keepdims=True)
        logs = log_ref[head, 0:1, pl.ds(start, WIDE)]
        dq = jnp.zeros((HDIM, WIDE), f32)
        for chunk in range(SEQ // WIDE):
            part = slice(chunk * WIDE, (chunk + 1) * WIDE)
            scores = lax.dot_general(
                k_s[part, :], query, (((1,), (1,)), ((), ())), preferred_element_type=f32
            )
            dprob = lax.dot_general(
                v_s[part, :], grad, (((1,), (1,)), ((), ())), preferred_element_type=f32
            )
            probs = jnp.exp2(scores * (FACTOR * LOG2E) - logs)
            dscore = (probs * (dprob - delta)).astype(bf16)
            dv_s[part, :] += jnp.dot(probs.astype(bf16), grad, preferred_element_type=f32)
            dk_s[part, :] += jnp.dot(dscore, query, preferred_element_type=f32)
            dq = dq + jnp.dot(kt_s[:, part], dscore, preferred_element_type=f32)
        dq_s[pl.ds(start, WIDE), :] = (dq.T * FACTOR).astype(bf16)
        return carry

    lax.fori_loop(0, SEQ // WIDE, step, 0)
    for key in range(CTX):
        rows = slice(key * ROWS, (key + 1) * ROWS)
        outs[key][:, :HDIM] = dq_s[rows, :]
        outs[key][:, HDIM : 2 * HDIM] = (dk_s[rows, :] * FACTOR).astype(bf16)
        outs[key][:, 2 * HDIM :] = dv_s[rows, :].astype(bf16)


def backward(head, pieces, att, grads, logs):
    return pl.pallas_call(
        lambda *refs: backward_body(head, *refs),
        in_specs=[VMEM] * (3 * CTX + 1),
        out_specs=[VMEM] * CTX,
        out_shape=[shape((ROWS, 3 * HDIM), bf16)] * CTX,
        scratch_shapes=[pltpu.VMEM((SEQ, HDIM), bf16)] * 4
        + [
            pltpu.VMEM((SEQ, HDIM), f32),
            pltpu.VMEM((HDIM, SEQ), bf16),
            pltpu.VMEM((SEQ, HDIM), bf16),
            pltpu.VMEM((SEQ, HDIM), f32),
            pltpu.VMEM((SEQ, HDIM), f32),
        ],
        compiler_params=params(24),
    )(*pieces, *att, *grads, logs)


def load_rows(table, arrays, runs, rows_s, sems):
    for place, (which, row) in enumerate(runs):
        target = pl.multiple_of(table[place], 32)
        block = lax.shift_right_logical(table[place], 8)
        pltpu.make_async_copy(
            arrays[which].at[pl.ds(row, 32), :], rows_s.at[pl.ds(target, 32), :], sems.at[block]
        ).start()


def wait_rows(key, rows_s, sems):
    rows = rows_s.at[pl.ds(pl.multiple_of(key * PIECE, PIECE), PIECE), :]
    pltpu.make_async_copy(rows, rows, sems.at[key]).wait()


def project_back_body(runs, table, own_ref, other_ref, *refs):
    arrays, refs = refs[:PARTS], refs[PARTS:]
    keep_ref, send_ref, rows_s, sems, grad_s = refs
    load_rows(table, arrays, runs, rows_s, sems)
    grad_s[0:ROWS, :] = own_ref[...]
    grad_s[ROWS:, :] = other_ref[...]

    def step(key, carry):
        wait_rows(key, rows_s, sems)
        out = lax.dot_general(
            grad_s[...],
            rows_s[pl.ds(pl.multiple_of(key * PIECE, PIECE), PIECE), :],
            (((1,), (1,)), ((), ())),
            preferred_element_type=f32,
        )
        keep_ref[key] = out[:ROWS]
        send_ref[key] = out[ROWS:].astype(bf16)
        return carry

    lax.fori_loop(0, CTX, step, 0)


def project_back(runs, table, own, other, arrays):
    return pl.pallas_call(
        lambda *refs: project_back_body(runs, *refs),
        in_specs=[SMEM, VMEM, VMEM] + [ANY] * PARTS,
        out_specs=[VMEM, VMEM],
        out_shape=[shape((CTX, ROWS, PIECE), f32), shape((CTX, ROWS, PIECE), bf16)],
        scratch_shapes=[
            pltpu.VMEM((HW, HALF), bf16),
            pltpu.SemaphoreType.DMA((CTX,)),
            pltpu.VMEM((2 * ROWS, HALF), bf16),
        ],
        compiler_params=params(32),
        name="project_back",
    )(table, own, other, *arrays)


def project_body(runs, table, *refs):
    own, other, refs = refs[0], refs[1], refs[2:]
    arrays, refs = refs[:PARTS], refs[PARTS:]
    keep_ref, send_ref, rows_s, sems, att_s, sum_s = refs
    load_rows(table, arrays, runs, rows_s, sems)
    for key in range(CTX):
        att_s[key, 0:ROWS, :] = own[key]
        att_s[key, ROWS:, :] = other[key]
    sum_s[...] = jnp.zeros_like(sum_s)

    def step(key, carry):
        wait_rows(key, rows_s, sems)
        sum_s[...] += jnp.dot(
            att_s[key],
            rows_s[pl.ds(pl.multiple_of(key * PIECE, PIECE), PIECE), :],
            preferred_element_type=f32,
        )
        return carry

    lax.fori_loop(0, CTX, step, 0)
    keep_ref[...] = sum_s[0:ROWS, :]
    send_ref[...] = sum_s[ROWS:, :].astype(bf16)


def project(runs, table, own, other, arrays):
    return pl.pallas_call(
        lambda *refs: project_body(runs, *refs),
        in_specs=[SMEM] + [VMEM] * 2 + [ANY] * PARTS,
        out_specs=[VMEM, VMEM],
        out_shape=[shape((ROWS, HALF), f32), shape((ROWS, HALF), bf16)],
        scratch_shapes=[
            pltpu.VMEM((HW, HALF), bf16),
            pltpu.SemaphoreType.DMA((CTX,)),
            pltpu.VMEM((CTX, 2 * ROWS, PIECE), bf16),
            pltpu.VMEM((2 * ROWS, HALF), f32),
        ],
        compiler_params=params(32),
        name="project",
    )(table, own, other, *arrays)


def stack_body(*refs):
    for key in range(CTX):
        refs[CTX][key] = refs[key][...]


def stack(pieces):
    return pl.pallas_call(
        stack_body,
        in_specs=[VMEM] * CTX,
        out_specs=VMEM,
        out_shape=shape((CTX, ROWS, PIECE), bf16),
        compiler_params=params(10),
        name="stack",
    )(*pieces)


def join_body(keep_ref, got_ref, *outs):
    for key in range(CTX):
        outs[key][...] = (keep_ref[key] + got_ref[key].astype(f32)).astype(bf16)


def join(keep, got):
    return pl.pallas_call(
        join_body,
        in_specs=[VMEM, VMEM],
        out_specs=[VMEM] * CTX,
        out_shape=[shape((ROWS, PIECE), bf16)] * CTX,
        compiler_params=params(10),
        name="join",
    )(keep, got)


COLS = 512
STEPS = HALF // COLS


def grad_proj_body(ids, *refs):
    ins, outs = refs[:8], refs[8:]
    for side in range(2):
        cot_ref, later_ref, gate_ref, conv_ref = ins[4 * side : 4 * side + 4]
        cot = cot_ref[...]
        ext = jnp.concatenate([cot, later_ref[...].astype(f32)], axis=0)
        grad = cot
        for offset in range(KSIZE):
            grad = grad + conv_ref[offset : offset + 1, :] * ext[offset * TOKF : offset * TOKF + ROWS]
        outs[side][...] = (gate_ref[...] * grad).astype(bf16)


def grad_proj(ids, cot, later, gate, conv):
    def spec(rows, side):
        return pl.BlockSpec((rows, COLS), lambda i, ids: (0, (ids[1] ^ side) * STEPS + i))

    ins = []
    for side in range(2):
        ins += [spec(ROWS, side), spec(SPAN, side), spec(1, side), spec(KSIZE, side)]
    return pl.pallas_call(
        grad_proj_body,
        grid_spec=pltpu.PrefetchScalarGridSpec(
            num_scalar_prefetch=1,
            grid=(STEPS,),
            in_specs=ins,
            out_specs=[pl.BlockSpec((ROWS, COLS), lambda i, ids: (0, i))] * 2,
        ),
        out_shape=[shape((ROWS, HALF), bf16)] * 2,
        compiler_params=params(16),
        name="grad_proj",
    )(ids, *([cot, later, gate, conv] * 2))


def mix_body(ids, resid_ref, gate_ref, keep_ref, got_ref, mixed_ref, tail_ref):
    near = pl.program_id(0) < STEPS
    projected = jnp.where(near, keep_ref[...], got_ref[...].astype(f32))
    mixed = (resid_ref[...] + gate_ref[...] * projected).astype(bf16)
    mixed_ref[...] = mixed
    tail_ref[...] = mixed[ROWS - SPAN :]


def mix(ids, resid, gate, keep, got):
    def full(i, ids):
        return (0, (ids[1] ^ (i // STEPS)) * STEPS + i % STEPS)

    return pl.pallas_call(
        mix_body,
        grid_spec=pltpu.PrefetchScalarGridSpec(
            num_scalar_prefetch=1,
            grid=(2 * STEPS,),
            in_specs=[
                pl.BlockSpec((ROWS, COLS), full),
                pl.BlockSpec((1, COLS), full),
                pl.BlockSpec((ROWS, COLS), lambda i, ids: (0, jnp.minimum(i, STEPS - 1))),
                pl.BlockSpec((ROWS, COLS), lambda i, ids: (0, jnp.maximum(i, STEPS) - STEPS)),
            ],
            out_specs=[pl.BlockSpec((ROWS, COLS), full), pl.BlockSpec((SPAN, COLS), full)],
        ),
        out_shape=[shape((ROWS, D), bf16), shape((SPAN, D), bf16)],
        compiler_params=params(16),
        name="mix",
    )(ids, resid, gate, keep, got)


def encode_body(mixed_ref, prior_ref, conv_ref, cot_ref, out_ref, sum_ref):
    mixed = mixed_ref[...].astype(f32)
    ext = jnp.concatenate([prior_ref[...].astype(f32), mixed], axis=0)
    cot = cot_ref[...]
    encoded = mixed
    for offset in range(KSIZE):
        begin = SPAN - offset * TOKF
        earlier = ext[begin : begin + ROWS]
        encoded = encoded + conv_ref[offset : offset + 1, :] * earlier
        row = offset * (D // COLS) + pl.program_id(0)
        sum_ref[pl.ds(row, 1), :] = jnp.sum(cot * earlier, axis=0, keepdims=True)
    out_ref[...] = encoded


def encode(mixed, prior, conv, cot):
    def spec(rows):
        return pl.BlockSpec((rows, COLS), lambda i: (0, i))

    return pl.pallas_call(
        encode_body,
        grid=(D // COLS,),
        in_specs=[spec(ROWS), spec(SPAN), spec(KSIZE), spec(ROWS)],
        out_specs=[spec(ROWS), pl.BlockSpec((KSIZE * D // COLS, COLS), lambda i: (0, 0))],
        out_shape=[shape((ROWS, D), f32), shape((KSIZE * D // COLS, COLS), f32)],
        compiler_params=params(16),
        name="encode",
    )(mixed, prior, conv, cot)


def unpack_body(ids, *refs):
    groups, outs = (refs[:CTX], refs[CTX : 2 * CTX]), refs[2 * CTX :]
    for key in range(CTX):
        for head, group in enumerate(groups):
            start = pl.multiple_of((ids[0] ^ key) * PIECE + head * HDIM, HDIM)
            for place in range(3):
                part = slice(place * HDIM, (place + 1) * HDIM)
                outs[place][:, pl.ds(start, HDIM)] = group[key][:, part]


def unpack(ids, firsts, seconds):
    return pl.pallas_call(
        unpack_body,
        in_specs=[SMEM] + [VMEM] * (2 * CTX),
        out_specs=[VMEM] * 3,
        out_shape=[shape((ROWS, HW), bf16)] * 3,
        compiler_params=params(12),
        name="unpack",
    )(ids, *firsts, *seconds)


def exchange(pieces, keys=range(1, CTX)):
    got = [swap(pieces[key], "ctx", key) for key in keys]
    return got if keys[0] > 1 else [pieces[0]] + got


def exchange_in(pieces, groups):
    got = []
    for keys in groups:
        got += exchange(pieces, range(*keys))
    return got


def after(values, *others):
    return lax.optimization_barrier((values, others))[0]


def add_swap(sums, axis, mask):
    return sums + swap(sums, axis, mask)


def block(queries, keys, values, resid, gate, out_weight, conv_weight, cotangent):
    ctx = lax.axis_index("ctx")
    fsdp = lax.axis_index("fsdp")
    core = fsdp % 2
    ids = jnp.stack([ctx, core]).astype(jnp.int32)

    other_rows = shift(out_weight, "core", 1)
    mine = lax.dynamic_slice(out_weight, (0, core * HALF), (16, HALF))
    theirs = lax.dynamic_slice(other_rows, (0, core * HALF), (16, HALF))
    rows = jnp.where(
        core == 0,
        jnp.concatenate([mine, theirs], axis=0),
        jnp.concatenate([theirs, mine], axis=0),
    )
    packed = pack(ids, queries[0], keys[0], values[0])
    gathered = gather_rows(rows)
    arrays = [g[0] for g in gathered]
    runs = []
    for which, (_, offs) in enumerate(gathered):
        for place, off in enumerate(offs):
            runs.append((off["z"] % 4, off["x"] % 2, which, place * 32, off))
    runs.sort(key=lambda run: run[:4])
    dx, dy, dz = (np.array([run[4][d] for run in runs], np.int32) for d in "xyz")
    x_lo, z = ctx // 4, ctx % 4
    x = (fsdp // 2 % 2) * 2 + x_lo
    run_x = (x + dx) % 4
    run_y = (fsdp // 4 + dy) % 4
    run_z = (z + dz) % 4
    block = ((run_x % 2) ^ x_lo) * 4 + (run_z ^ z)
    table = (block * PIECE + run_y * 64 + (run_x // 2) * 32).astype(jnp.int32)
    runs = [run[2:4] for run in runs]

    pieces = exchange(packed, range(1, 4))
    pieces += exchange(packed, range(4, CTX))
    later = along(cotangent[0, :SPAN].astype(bf16), -1)
    results = forward(after(pieces, arrays[0], arrays[1]))
    att, logs = results[:CTX], results[CTX]
    own_att = exchange(att)
    own_grad, send_grad = grad_proj(ids, cotangent[0], later, gate, conv_weight)
    other_grad = shift(send_grad, "core", 1)
    keep, send = project_back(runs, table, own_grad, other_grad, arrays)
    got = shift(send, "core", 1)
    own_att = stack(own_att)
    other_att = shift(own_att, "core", 1)
    joined = join(keep, got)
    grads = exchange(joined)

    keep, send = project(runs, table, after(own_att, joined[0]), other_att, arrays)
    mixed, tail = mix(ids, resid[0], gate, keep, shift(send, "core", 1))
    prior = along(tail, 1)

    firsts = backward(0, pieces, att, after(grads, tail), logs)
    encoded, sums = encode(mixed, prior, conv_weight, after(cotangent[0], firsts[0]))
    sums = add_swap(sums, "fsdp", 1)
    early = exchange_in(firsts, ((1, 4), (4, 8)))
    sums = add_swap(sums, "fsdp", 4)
    seconds = backward(1, pieces, att, grads, logs)
    sums = add_swap(after(sums, seconds[0]), "fsdp", 8)
    sums = add_swap(sums, "fsdp", 2)
    late = exchange_in(seconds, ((1, 3), (3, 5), (5, 7), (7, 8)))
    sums = add_swap(sums, "ctx", 4)
    sums = add_swap(sums, "ctx", 1)
    last = swap(sums, "ctx", 2)
    grad_q, grad_k, grad_v = unpack(ids, early, late)
    sums = sums + after(last, grad_q)
    grad_conv = sums.reshape(KSIZE, D)
    return (encoded[None], grad_q[None], grad_k[None], grad_v[None], grad_conv)


def solution(mesh):
    token = P("fsdp", "ctx", None)
    in_specs = (
        token,
        token,
        token,
        token,
        P("fsdp", None),
        P(("ctx", "fsdp"), None),
        P(),
        token,
    )
    return jax.shard_map(
        block,
        mesh=mesh,
        in_specs=in_specs,
        out_specs=(token, token, token, token, P()),
        check_vma=False,
    )
```
